32 devices in a mesh: dp: 8 (over z, x), tensor: 4 (over y, core).
Axes of the slice: x: 2, y: 2, z: 4, core: 2. Of those that a mesh axis runs over, the one named last changes fastest.
Arguments:
- source_rows: bfloat16 [2, 2048, 3072], P(None, ('dp', 'tensor')), may hold values from -6 to 6
- gate_weight: bfloat16 [2, 3072, 9216], P(None, 'dp', 'tensor'), may hold values from -0.15625 to 0.15625
- up_weight: bfloat16 [2, 3072, 9216], P(None, 'dp', 'tensor'), may hold values from -0.15625 to 0.15625
- keep_mask: int32 [2, 2, 48, 144], replicated, may hold values from 0 to 1, as said below
Outputs:
- hidden: bfloat16 [2, 2048, 9216], P(None, 'dp', 'tensor')
The draws below stay inside these ranges and needn't reach their ends.
Inputs may be any that keep to these rules, and one draw needn't show every extreme that they name: `keep_mask`: within each device's share of a projection (6 x 36 blocks: block rows of one dp index, block columns of one tensor index) at least one and at most 108 blocks are kept, and for each direction and projection some share keeps exactly 108.
All inputs are finite; a program needn't handle non-finite values.
Results may differ from the reference program's by a relative error of at most 0.001.
Values may be sent and summed in bfloat16 or wider, within the bound.
No kernel may reach another device: no remote copies, remote signals or barrier semaphores. Data moves between devices by JAX's collectives and lax.ppermute only.
A program may use at most 192 MiB of HBM per device.

```python
import jax
import jax.numpy as jnp
from jax import lax

D = 3072
FF = 9216
BLOCK = 64
TOK_DEV = 64
TOKENS = 2048
DB_DEV = 6
FB_DEV = 36
CAP = 108
N_DP = 8
N_TENSOR = 4


def draw_keep_mask(key, part):
    shard_total = N_DP * N_TENSOR
    cell_count = DB_DEV * FB_DEV
    key_count, key_chosen, key_order = jax.random.split(key, 3)
    counts = jax.random.randint(key_count, (4, shard_total), (CAP + 1) // 2, CAP + 1)
    chosen = jax.random.randint(key_chosen, (4, 1), 0, shard_total)
    counts = jnp.where(jnp.arange(shard_total)[None, :] == chosen, CAP, counts)
    order_keys = jax.random.split(key_order, 4 * shard_total)

    def shuffled(single_key):
        return jax.random.permutation(single_key, cell_count)
    ranks = jax.vmap(shuffled)(order_keys).reshape(4, shard_total, cell_count)
    keeping = (ranks < counts[:, :, None]).astype(jnp.int32)
    keeping = keeping.reshape(2, 2, N_DP, N_TENSOR, DB_DEV, FB_DEV).transpose(0, 1, 2, 4, 3, 5)
    return keeping.reshape(2, 2, DB_DEV * N_DP, FB_DEV * N_TENSOR)


def steps_of(stream_key, dims, pieces, least, top_value):
    loudness = 1.0
    for dim, blocks in pieces:
        draws = jax.random.uniform(jax.random.fold_in(jax.random.fold_in(stream_key, 6), dim), (blocks,), jnp.float32, least / len(pieces), top_value / len(pieces))
        loudness = loudness * jnp.repeat(jnp.exp(draws), dims[dim] // blocks).reshape((-1,) + (1,) * (len(dims) - 1 - dim))
    return loudness


def normal_values(key, extent, deviation, limit, cuts=(), dtype=jnp.bfloat16):
    result = deviation * jax.random.normal(key, extent, jnp.float32)
    if cuts:
        result = result * steps_of(key, extent, cuts, -0.22, 0.18)
    return jnp.clip(result, -limit, limit).astype(dtype)


def setup_inputs(seed: int = 0) -> dict:
    splits = jax.random.split(jax.random.key(seed), 5)
    return {
        "source_rows": normal_values(splits[0], (2, TOKENS, D), 1.0, 6.0, ((1, 32),)),
        "gate_weight": normal_values(splits[1], (2, D, FF), (D // 2) ** -0.5, 0.15625, ((1, 8), (2, 4))),
        "up_weight": normal_values(splits[2], (2, D, FF), (D // 2) ** -0.5, 0.15625, ((1, 8), (2, 4))),
        "keep_mask": draw_keep_mask(jax.random.fold_in(splits[4], 71), 0),
    }


def reference(source_rows, gate_weight, up_weight, keep_mask):
    results = []
    for model_index in range(2):
        gate_mask = jnp.repeat(jnp.repeat(keep_mask[model_index, 0], BLOCK, axis=0), BLOCK, axis=1)
        up_mask = jnp.repeat(jnp.repeat(keep_mask[model_index, 1], BLOCK, axis=0), BLOCK, axis=1)
        gate_kept = gate_weight[model_index] * gate_mask.astype(jnp.bfloat16)
        up_kept = up_weight[model_index] * up_mask.astype(jnp.bfloat16)

        def one_block(token_block):
            gate_sum = jnp.dot(token_block, gate_kept, preferred_element_type=jnp.float32)
            up_sum = jnp.dot(token_block, up_kept, preferred_element_type=jnp.float32)
            return (jax.nn.silu(gate_sum) * up_sum).astype(jnp.bfloat16)

        token_blocks = source_rows[model_index].reshape(N_DP, TOK_DEV * N_TENSOR, D)
        mapped = lax.map(one_block, token_blocks)
        results.append(mapped.reshape(TOKENS, FF))
    return jnp.stack(results, axis=0)
```

```python
import functools

import jax
import jax.numpy as jnp
from jax import lax
from jax.experimental import pallas as pl
from jax.experimental.pallas import tpu as pltpu
from jax.sharding import PartitionSpec as P

BLOCK = 64
HALF = BLOCK // 2
LANES = 128
TILE = 256
PER_TILE = TILE // BLOCK
AXES = ("dp", "tensor")


def expand_blocks(block_mask, block_width):
    return jnp.repeat(jnp.repeat(block_mask, block_width, axis=-2), block_width, axis=-1)


def plain_shards(source_rows, gate_weight, up_weight, keep_mask):
    token_slab = lax.all_gather(source_rows, "tensor", axis=1, tiled=True)
    row_blocks = gate_weight.shape[1] // BLOCK
    col_blocks = gate_weight.shape[2] // BLOCK
    dp_index = lax.axis_index("dp")
    tensor_index = lax.axis_index("tensor")
    mask_cols = lax.dynamic_slice_in_dim(keep_mask, tensor_index * col_blocks, col_blocks, 3)
    own_mask = lax.dynamic_slice_in_dim(mask_cols, dp_index * row_blocks, row_blocks, 2)
    stacked = jnp.stack([gate_weight, up_weight], axis=1)
    kept_rows = stacked * expand_blocks(own_mask, BLOCK).astype(jnp.bfloat16)
    weights = lax.all_gather(kept_rows, "dp", axis=2, tiled=True)
    gate_sum = jnp.einsum(
        "mgd,mdf->mgf", token_slab, weights[:, 0], preferred_element_type=jnp.float32
    )
    up_sum = jnp.einsum(
        "mgd,mdf->mgf", token_slab, weights[:, 1], preferred_element_type=jnp.float32
    )
    return (jax.nn.silu(gate_sum) * up_sum).astype(jnp.bfloat16)


def turn(v):
    return pltpu.roll(v, LANES // 2, 1)


def left_half():
    return lax.broadcasted_iota(jnp.int32, (HALF, LANES), 1) < LANES // 2


def pack_body(row_blocks, cap, mask, gate, up, gate_out, up_out, slots, count, sems):
    j = pl.program_id(0)

    @pl.when(j == 0)
    def _():
        count[0] = 0
        count[1] = 0

    left = left_half()
    for p, ref in enumerate((gate, up)):
        n = count[p]
        for r in range(row_blocks):
            for c in range(PER_TILE):
                lanes = pl.ds((c // 2) * LANES, LANES)
                odd = c % 2
                stay = ref[0, pl.ds(r * BLOCK + odd * HALF, HALF), lanes]
                move = turn(ref[0, pl.ds(r * BLOCK + (1 - odd) * HALF, HALF), lanes])
                v = jnp.where(left, move, stay) if odd else jnp.where(left, stay, move)
                slots[p, pl.ds(pl.multiple_of(n * HALF, HALF), HALF), :] = v
                n = n + mask[p, r, j * PER_TILE + c]
        count[p] = n

    @pl.when(j == pl.num_programs(0) - 1)
    def _():
        copies = [
            pltpu.make_async_copy(slots.at[p, pl.ds(0, cap * HALF)], out, sems.at[p])
            for p, out in enumerate((gate_out, up_out))
        ]
        for copy in copies:
            copy.start()
        for copy in copies:
            copy.wait()


def pack(m, mask, gate_weight, up_weight):
    _, rows, cols = gate_weight.shape
    row_blocks = rows // BLOCK
    cap = row_blocks * (cols // BLOCK) // 2
    piece = jax.ShapeDtypeStruct((cap * HALF, LANES), jnp.bfloat16)
    spec = pl.BlockSpec((1, rows, TILE), lambda j, mask: (m, 0, j))
    return pl.pallas_call(
        functools.partial(pack_body, row_blocks, cap),
        out_shape=(piece, piece),
        grid_spec=pltpu.PrefetchScalarGridSpec(
            num_scalar_prefetch=1,
            grid=(cols // TILE,),
            in_specs=[spec, spec],
            out_specs=[pl.BlockSpec(memory_space=pl.ANY)] * 2,
            scratch_shapes=[
                pltpu.VMEM((2, (cap + 1) * HALF, LANES), jnp.bfloat16),
                pltpu.SMEM((2,), jnp.int32),
                pltpu.SemaphoreType.DMA((2,)),
            ],
        ),
        cost_estimate=pl.CostEstimate(flops=0, bytes_accessed=6 * rows * cols, transcendentals=0),
        name="pack_kept",
    )(mask, gate_weight, up_weight)


def mix_body(m, shares, rows, cap, first, last, place, mask, near, far, *refs):
    packs = refs[: 2 * shares]
    refs = refs[2 * shares :]
    before = None
    if not first:
        before, refs = refs[0], refs[1:]
    out, held, dense, x, count, sems = refs
    j = pl.program_id(0)
    row_blocks = rows // BLOCK
    tokens = near.shape[2]

    @pl.when(j == 0)
    def _():
        copies = []
        for s in range(shares):
            for p in range(2):
                copies.append(
                    pltpu.make_async_copy(
                        packs[2 * s + p],
                        held.at[2 * s + p, pl.ds(0, cap * HALF)],
                        sems.at[len(copies)],
                    )
                )
            columns = pl.ds(pl.multiple_of(place[s] * rows, LANES), rows)
            for k in range(4):
                source = near if k < 2 else far
                at = pl.ds(pl.multiple_of(place[shares + k] * tokens, tokens), tokens)
                copies.append(
                    pltpu.make_async_copy(
                        source.at[k % 2, m, :, columns],
                        x.at[at, pl.ds(s * rows, rows)],
                        sems.at[len(copies)],
                    )
                )
        for copy in copies:
            copy.start()
        for k in range(2 * shares):
            held[k, pl.ds(cap * HALF, HALF), :] = jnp.zeros((HALF, LANES), jnp.bfloat16)
            count[k] = 0
        for copy in copies:
            copy.wait()

    left = left_half()
    for s in range(shares):
        top = place[s] * row_blocks
        for p in range(2):
            k = 2 * s + p
            n = count[k]
            for r in range(row_blocks):
                for c in range(0, PER_TILE, 2):
                    keep_a = mask[p, top + r, j * PER_TILE + c]
                    keep_b = mask[p, top + r, j * PER_TILE + c + 1]
                    at_a = jnp.where(keep_a > 0, n, cap)
                    at_b = jnp.where(keep_b > 0, n + keep_a, cap)
                    n = n + keep_a + keep_b
                    a = held[k, pl.ds(pl.multiple_of(at_a * HALF, HALF), HALF), :]
                    b = held[k, pl.ds(pl.multiple_of(at_b * HALF, HALF), HALF), :]
                    lanes = pl.ds((c // 2) * LANES, LANES)
                    at = s * rows + r * BLOCK
                    dense[p, pl.ds(at, HALF), lanes] = jnp.where(left, a, turn(b))
                    dense[p, pl.ds(at + HALF, HALF), lanes] = jnp.where(left, turn(a), b)
            count[k] = n

    sums = [jnp.dot(x[...], dense[p], preferred_element_type=jnp.float32) for p in range(2)]
    if not first:
        sums = [before[p] + sums[p] for p in range(2)]
    if last:
        out[...] = (jax.nn.silu(sums[0]) * sums[1]).astype(out.dtype)
    else:
        for p in range(2):
            out[p] = sums[p]


def mix(m, place, mask, near, far, packs, before, last, rows, cols):
    shares = len(packs) // 2
    cap = (rows // BLOCK) * (cols // BLOCK) // 2
    group = 4 * near.shape[2]
    first = before is None
    sums = pl.BlockSpec((2, group, TILE), lambda j, place, mask: (0, 0, j))
    whole = pl.BlockSpec(memory_space=pl.ANY)
    if last:
        out_shape = jax.ShapeDtypeStruct((group, cols), jnp.bfloat16)
        out_spec = pl.BlockSpec((group, TILE), lambda j, place, mask: (0, j))
    else:
        out_shape = jax.ShapeDtypeStruct((2, group, cols), jnp.float32)
        out_spec = sums
    return pl.pallas_call(
        functools.partial(mix_body, m, shares, rows, cap, first, last),
        out_shape=out_shape,
        grid_spec=pltpu.PrefetchScalarGridSpec(
            num_scalar_prefetch=2,
            grid=(cols // TILE,),
            in_specs=[whole] * (2 + 2 * shares) + ([] if first else [sums]),
            out_specs=out_spec,
            scratch_shapes=[
                pltpu.VMEM((2 * shares, (cap + 1) * HALF, LANES), jnp.bfloat16),
                pltpu.VMEM((2, shares * rows, TILE), jnp.bfloat16),
                pltpu.VMEM((group, shares * rows), jnp.bfloat16),
                pltpu.SMEM((2 * shares,), jnp.int32),
                pltpu.SemaphoreType.DMA((6 * shares,)),
            ],
        ),
        cost_estimate=pl.CostEstimate(
            flops=4 * group * shares * rows * cols,
            bytes_accessed=4 * shares * rows * cols + 16 * group * cols,
            transcendentals=0,
        ),
        name="mix_last" if last else "mix",
    )(place, mask, near, far, *packs, *([] if first else [before]))


def shards(n_dp, n_tensor, source_rows, gate_weight, up_weight, keep_mask):
    _, rows, cols = gate_weight.shape
    row_blocks = rows // BLOCK
    col_blocks = cols // BLOCK
    dp = lax.axis_index("dp")
    tensor = lax.axis_index("tensor")

    def moved(to):
        pairs = []
        for d in range(n_dp):
            for t in range(n_tensor):
                zh, zl, xx, yy, cc = to(d // 4, (d // 2) % 2, d % 2, t // 2, t % 2)
                pairs.append((d * n_tensor + t, ((zh * 2 + zl) * 2 + xx) * n_tensor + yy * 2 + cc))
        return lambda v: lax.ppermute(v, AXES, pairs)

    over_core = moved(lambda zh, zl, x, y, c: (zh, zl, x, y, 1 - c))
    over_x = moved(lambda zh, zl, x, y, c: (zh, zl, 1 - x, y, c))
    over_y = moved(lambda zh, zl, x, y, c: (zh, zl, x, 1 - y, c))
    over_zh = moved(lambda zh, zl, x, y, c: (1 - zh, zl, x, y, c))
    traded = moved(lambda zh, zl, x, y, c: (zh, c, x, y, zl))

    zh, zl, x = dp // 4, (dp // 2) % 2, dp % 2
    y, c = tensor // 2, tensor % 2
    slice_at = (y * 2 + zl) * col_blocks

    own_mask = lax.dynamic_slice(
        keep_mask, (0, 0, dp * row_blocks, tensor * col_blocks), (2, 2, row_blocks, col_blocks)
    )
    slice_mask = lax.dynamic_slice_in_dim(keep_mask, slice_at, col_blocks, 3)

    def index_of(zh, zl, x):
        return (zh * 2 + zl) * 2 + x

    pieces = [y * 2 + zl, y * 2 + 1 - zl, (1 - y) * 2 + zl, (1 - y) * 2 + 1 - zl]

    def place_of(zh, x):
        ids = [index_of(zh, c, x), index_of(zh, 1 - c, x)]
        return jnp.stack(ids + pieces).astype(jnp.int32)

    chip_rows = jnp.stack([source_rows, over_core(source_rows)])
    near = traded(chip_rows)
    far = over_y(near)

    packed = [pack(m, own_mask[m], gate_weight, up_weight) for m in range(2)]
    outs = []
    for m in range(2):
        home = [traded(v) for v in packed[m]]
        other = [over_zh(v) for v in home]
        home_x = [over_x(v) for v in home]
        other_x = [over_x(v) for v in other]
        sums = None
        steps = [(home, zh, x), (home_x, zh, 1 - x), (other, 1 - zh, x), (other_x, 1 - zh, 1 - x)]
        for i, (have, at_zh, at_x) in enumerate(steps):
            both = have + [over_core(v) for v in have]
            sums = mix(
                m, place_of(at_zh, at_x), slice_mask[m], near, far, both, sums, i == 3, rows, cols
            )
        outs.append(traded(sums))
    return jnp.stack(outs)


def solution(mesh):
    placed = (
        P(None, ("dp", "tensor"), None),
        P(None, "dp", "tensor"),
        P(None, "dp", "tensor"),
        P(),
    )
    n_dp, n_tensor = mesh.shape["dp"], mesh.shape["tensor"]

    def step(source_rows, gate_weight, up_weight, keep_mask):
        rows = gate_weight.shape[1] // n_dp
        cols = gate_weight.shape[2] // n_tensor
        fits = n_dp == 8 and n_tensor == 4 and cols % TILE == 0 and rows % LANES == 0
        body = functools.partial(shards, n_dp, n_tensor) if fits else plain_shards
        return jax.shard_map(
            body, mesh=mesh, in_specs=placed, out_specs=P(None, "dp", "tensor"), check_vma=False
        )(source_rows, gate_weight, up_weight, keep_mask)

    return step
```
